32 devices in a mesh: dp: 8 (over y, x, core), vocab: 4 (over z).
Axes of the slice: x: 2, y: 2, z: 4, core: 2. Of those that a mesh axis runs over, the one named last changes fastest.
Arguments:
- hidden: bfloat16 [3840, 4096], P('dp', 'vocab'), may hold values from -8 to 8
- head: bfloat16 [4096, 2048], P(None, 'vocab'), may hold values from -3 to 3
- shortlist: int32 [16, 8], P('dp', 'vocab'), may hold values from 0 to 1, as said below
- tokens: int32 [3840], P('dp'), may hold values from 0 to 2047, as said below
- risk: int32 [16, 12], P('dp'), may hold values from 0 to 100
Outputs:
- hidden_grad: bfloat16 [3840, 4096], P(('dp', 'vocab'))
- head_grad: float32 [4096, 2048], P('dp', 'vocab')
- expected: float32 [16], P('dp')
The draws below stay inside these ranges and needn't reach their ends.
Inputs may be any that keep to these rules, and one draw needn't show every extreme that they name: Every sentence's shortlist holds at least one block. `tokens`: each token's word lies in a block that its sentence's shortlist holds.
All inputs are finite; a program needn't handle non-finite values.
Results may differ from the reference program's by a relative error of at most 0.013.
Values may be sent and summed in bfloat16 or wider, within the bound.
No kernel may reach another device: no remote copies, remote signals or barrier semaphores. Data moves between devices by JAX's collectives and lax.ppermute only.
A program may use at most 64 MiB of HBM per device.

```python
import math
import jax
import jax.numpy as jnp
from jax import lax

D = 4096
BLK = 256
CANDS = 12
LEN = 20
BLOCKS = 8
WROWS = 2048
SENTS = 16
TOKENS = 3840
N_DP = 8
N_VOCAB = 4


def routing(key):
    base = jax.random.fold_in(key, 11)
    key_weight, key_draw, key_forced, key_pick, key_word = jax.random.split(base, 5)
    popularity = jax.random.randint(key_weight, (BLOCKS,), 1, 9)
    rolled = jax.random.randint(key_draw, (SENTS, BLOCKS), 0, 8)
    forced = jax.random.randint(key_forced, (SENTS,), 0, BLOCKS)
    listed = (rolled < popularity[None, :]) | (jnp.arange(BLOCKS)[None, :] == forced[:, None])
    listed = listed.astype(jnp.int32)
    listed_count = jnp.sum(listed, axis=1)
    sentence = jnp.arange(TOKENS) // (CANDS * LEN)
    picked = jax.random.randint(key_pick, (TOKENS,), 0, 1 << 20) % listed_count[sentence]
    running = jnp.cumsum(listed, axis=1)[sentence]
    block_index = jnp.sum((running <= picked[:, None]).astype(jnp.int32), axis=1)
    words = jax.random.randint(key_word, (TOKENS,), 0, BLK)
    return (listed, (block_index * BLK + words).astype(jnp.int32))


def head_matrix(key):
    base = jax.random.fold_in(key, 23)
    spread = 3.0 / math.sqrt(D)
    matrix = jax.random.normal(base, (D, WROWS), jnp.float32) * spread
    return jnp.clip(matrix, -6.0 * spread, 6.0 * spread)


def draw_shortlist(key, part):
    return routing(key)[0]


def draw_tokens(key, part):
    return routing(key)[1]


def draw_head(key, part):
    return head_matrix(key).astype(jnp.bfloat16)


def draw_hidden(key, part):
    base = jax.random.fold_in(key, 31)
    values = jax.random.normal(base, (TOKENS, D), jnp.float32)
    return jnp.clip(values, -8.0, 8.0).astype(jnp.bfloat16)


def set_ends(result, own_key, smallest, high):
    longest = result.shape.index(max(result.shape))
    spots = []
    for shift in (0, 1):
        where = [jax.random.randint(jax.random.fold_in(own_key, axis), (), 0, length) for axis, length in enumerate(result.shape)]
        where[longest] = (where[longest] + shift) % result.shape[longest]
        spots.append(tuple(where))
    return result.at[spots[0]].set(smallest).at[spots[1]].set(high)


def setup_inputs(seed: int = 0) -> dict:
    key_list = jax.random.split(jax.random.key(seed), 6)
    hidden = draw_hidden(jax.random.fold_in(key_list[5], 71), 0)
    head = draw_head(jax.random.fold_in(key_list[5], 71), 0)
    shortlist = draw_shortlist(jax.random.fold_in(key_list[5], 71), 0)
    tokens = draw_tokens(jax.random.fold_in(key_list[5], 71), 0)
    risk = set_ends(jax.random.randint(key_list[4], (SENTS, CANDS), 0, 101), jax.random.fold_in(key_list[4], 1), 0, 100).astype(jnp.int32)
    return {"hidden": hidden, "head": head, "shortlist": shortlist, "tokens": tokens, "risk": risk}


masked_value = -1e30
loss_scale = 2048.0


def reference(hidden, head, shortlist, tokens, risk):
    logits = jnp.dot(hidden, head, preferred_element_type=jnp.float32)
    per_sentence = CANDS * LEN
    expanded = jnp.repeat(shortlist, BLK, axis=1) == 1
    allowed = jnp.repeat(expanded, per_sentence, axis=0)
    masked = jnp.where(allowed, logits, masked_value)
    row_peak = jnp.max(masked, axis=1)
    shifted = jnp.where(allowed, jnp.exp(masked - row_peak[:, None]), 0.0)
    row_total = jnp.sum(shifted, axis=1)
    chosen = jnp.take_along_axis(logits, tokens[:, None].astype(jnp.int32), axis=1)[:, 0]
    logprob = chosen - row_peak - jnp.log(row_total)
    scores = jnp.mean(logprob.reshape(SENTS, CANDS, LEN), axis=2)
    raised = jnp.exp(scores)
    weights = raised / jnp.sum(raised, axis=1, keepdims=True)
    cost_value = risk.astype(logits.dtype) / 100.0
    expected = jnp.sum(weights * cost_value, axis=1)
    cand_coeff = loss_scale * weights * (cost_value - expected[:, None]) / LEN
    row_coeff = jnp.repeat(cand_coeff.reshape(SENTS * CANDS), LEN)
    row_prob = shifted / row_total[:, None]
    target_hit = tokens[:, None] == jnp.arange(WROWS, dtype=jnp.int32)[None, :]
    grad_logits = (row_coeff[:, None] * (target_hit.astype(logits.dtype) - row_prob)).astype(jnp.bfloat16)
    group_cols = WROWS // N_VOCAB
    hidden_grad = jnp.zeros((TOKENS, D), jnp.float32)
    for group in range(N_VOCAB):
        part_grad = grad_logits[:, group * group_cols:(group + 1) * group_cols]
        part_head = head[:, group * group_cols:(group + 1) * group_cols]
        partial_value = jnp.dot(part_grad, part_head.T, preferred_element_type=jnp.float32)
        rounded = lax.optimization_barrier(partial_value.astype(jnp.bfloat16))
        hidden_grad = hidden_grad + rounded.astype(hidden_grad.dtype)
    group_rows = TOKENS // N_DP
    head_grad = jnp.zeros((D, WROWS), jnp.float32)
    for group in range(N_DP):
        part_hidden = hidden[group * group_rows:(group + 1) * group_rows]
        part_grad = grad_logits[group * group_rows:(group + 1) * group_rows]
        partial_value = jnp.dot(part_hidden.T, part_grad, preferred_element_type=jnp.float32)
        rounded = lax.optimization_barrier(partial_value.astype(jnp.bfloat16))
        head_grad = head_grad + rounded.astype(head_grad.dtype)
    return hidden_grad.astype(jnp.bfloat16), head_grad, expected
```

```python
import jax
import jax.numpy as jnp
from jax import lax
from jax.sharding import PartitionSpec as P


masked_value = -1e30
loss_scale = 2048.0


def add_pieces(received):
    return jnp.sum(received.astype(jnp.float32), axis=0)


def swap_dp(value, bit):
    count = lax.axis_size("dp")
    return lax.ppermute(value, "dp", [(i, i ^ bit) for i in range(count)])


def shift_half(value):
    count = lax.axis_size("vocab")
    return lax.ppermute(value, "vocab", [(i, (i + count // 2) % count) for i in range(count)])


def shift_within(value, step):
    count = lax.axis_size("vocab")
    group = count // 2
    pairs = [(i, i // group * group + (i % group + step) % group) for i in range(count)]
    return lax.ppermute(value, "vocab", pairs)


def dp_bits():
    count = lax.axis_size("dp")
    return [1 << b for b in range(count.bit_length() - 1)]


def bit_axis(bit):
    return len(dp_bits()) - bit.bit_length()


def my_bit(bit):
    return (lax.axis_index("dp") // bit) % 2


def gather_step(held, bit):
    received = swap_dp(held, bit)
    axis = bit_axis(bit)
    shape = list(held.shape)
    shape[axis] = 2
    place = lax.broadcasted_iota(jnp.int32, shape, axis)
    return jnp.where(place == my_bit(bit), held, received)


def gather_dp(piece, orders):
    bits = dp_bits()
    count = len(orders)
    width = piece.shape[1] // count
    parts = []
    for index, order in enumerate(orders):
        held = piece[:, index * width : (index + 1) * width]
        held = held.reshape((1,) * len(bits) + held.shape)
        for bit in order:
            held = gather_step(held, bit)
        parts.append(held.reshape(-1, width))
    return parts


def scatter_step(total, bit):
    axis = bit_axis(bit)
    mine = my_bit(bit)
    keep = lax.dynamic_slice_in_dim(total, mine, 1, axis)
    send = lax.dynamic_slice_in_dim(total, 1 - mine, 1, axis).astype(jnp.bfloat16)
    return keep + swap_dp(send, bit).astype(jnp.float32)


def plain(hidden, head, shortlist, tokens, risk):
    features = lax.all_gather(hidden, "vocab", axis=1, tiled=True)
    row_count = features.shape[0]
    sent_count = shortlist.shape[0]
    cand_count = risk.shape[1]
    per_sentence = row_count // sent_count
    seq_length = per_sentence // cand_count
    col_count = head.shape[1]
    block_width = col_count // shortlist.shape[1]
    col_offset = lax.axis_index("vocab") * col_count
    expanded = jnp.repeat(shortlist, block_width, axis=1) == 1
    allowed = jnp.broadcast_to(expanded[:, None, :], (sent_count, per_sentence, col_count)).reshape(
        row_count, col_count
    )
    target_hit = (tokens - col_offset)[:, None] == jnp.arange(col_count, dtype=jnp.int32)[None, :]
    logits = jnp.dot(features, head, preferred_element_type=jnp.float32)
    masked = jnp.where(allowed, logits, masked_value)
    row_peak = jnp.max(masked, axis=1)
    row_total = jnp.sum(jnp.where(allowed, jnp.exp(masked - row_peak[:, None]), 0.0), axis=1)
    chosen = jnp.sum(jnp.where(target_hit, logits, 0.0), axis=1)
    global_peak = lax.pmax(row_peak, "vocab")
    global_total, target_logit = lax.psum(
        (row_total * jnp.exp(row_peak - global_peak), chosen), "vocab"
    )
    logprob = target_logit - global_peak - jnp.log(global_total)
    expected, cand_coeff = candidate_terms(logprob, risk, seq_length)
    row_coeff = jnp.broadcast_to(
        cand_coeff[:, :, None], (sent_count, cand_count, seq_length)
    ).reshape(row_count)
    row_prob = (
        jnp.where(allowed, jnp.exp(masked - global_peak[:, None]), 0.0) / global_total[:, None]
    )
    grad_logits = (row_coeff[:, None] * (target_hit.astype(jnp.float32) - row_prob)).astype(
        jnp.bfloat16
    )
    model_width = features.shape[1]
    vocab_count = lax.axis_size("vocab")
    share_rows = row_count // vocab_count
    partial_value = (
        lax.dot_general(
            grad_logits, head, (((1,), (1,)), ((), ())), preferred_element_type=jnp.float32
        )
        .astype(jnp.bfloat16)
        .reshape(vocab_count, share_rows, model_width)
    )
    summed = add_pieces(
        lax.all_to_all(partial_value, "vocab", split_axis=0, concat_axis=0, tiled=True)
    )
    head_grad = lax.psum_scatter(
        lax.dot_general(
            features, grad_logits, (((0,), (0,)), ((), ())), preferred_element_type=jnp.float32
        ).astype(jnp.bfloat16),
        "dp",
        scatter_dimension=0,
        tiled=True,
    ).astype(jnp.float32)
    return (summed.astype(jnp.bfloat16), head_grad, expected)


def candidate_terms(logprob, risk, seq_length):
    sent_count, cand_count = risk.shape
    scores = jnp.mean(logprob.reshape(sent_count, cand_count, seq_length), axis=2)
    raised = jnp.exp(scores)
    weights = raised / jnp.sum(raised, axis=1, keepdims=True)
    cost_value = risk.astype(jnp.float32) / 100.0
    expected = jnp.sum(weights * cost_value, axis=1)
    coeff = loss_scale * weights * (cost_value - expected[:, None]) / seq_length
    return expected, coeff


def halves(hidden, head, shortlist, tokens, risk):
    vocab_count = lax.axis_size("vocab")
    group = vocab_count // 2
    dp_count = lax.axis_size("dp")
    place = lax.axis_index("vocab")
    half = place // group
    spot = place % group
    row_count = hidden.shape[0] // 2
    slice_width = hidden.shape[1]
    model_width, col_count = head.shape
    sent_count = shortlist.shape[0] // 2
    cand_count = risk.shape[1]
    seq_length = row_count // sent_count // cand_count
    block_width = col_count // shortlist.shape[1]
    other = (place + group) % vocab_count
    bits = dp_bits()
    wide = bits[1:]
    orders = (wide + [1], wide[::-1] + [1])

    piece_rows = model_width // dp_count
    piece = lax.dynamic_slice_in_dim(head, lax.axis_index("dp") * piece_rows, piece_rows, 0)
    far_parts = gather_dp(shift_half(piece), orders)
    far_head = jnp.concatenate(far_parts, axis=1)

    own_rows = lax.dynamic_slice_in_dim(hidden, half * row_count, row_count, 0)
    far_rows = lax.dynamic_slice_in_dim(hidden, (1 - half) * row_count, row_count, 0)
    crossed = shift_half(far_rows)
    features = jnp.zeros((row_count, model_width), jnp.bfloat16)

    def put(features, block, index):
        return lax.dynamic_update_slice_in_dim(features, block, index * slice_width, 1)

    features = put(features, own_rows, place)
    features = put(features, crossed, other)
    for step in range(1, group):
        source = half * group + (spot - step) % group
        features = put(features, shift_within(own_rows, step), source)
        features = put(
            features, shift_within(crossed, step), (source + group) % vocab_count
        )

    own_list = lax.dynamic_slice_in_dim(shortlist, half * sent_count, sent_count, 0)
    far_list = shift_half(
        lax.dynamic_slice_in_dim(shortlist, (1 - half) * sent_count, sent_count, 0)
    )
    words = lax.dynamic_slice_in_dim(tokens, half * row_count, row_count, 0)
    costs = lax.dynamic_slice_in_dim(risk, half * sent_count, sent_count, 0)

    def view(head_part, listed, index):
        expanded = jnp.repeat(listed, block_width, axis=1) == 1
        allowed = jnp.broadcast_to(
            expanded[:, None, :], (sent_count, row_count // sent_count, col_count)
        ).reshape(row_count, col_count)
        hit = (words - index * col_count)[:, None] == jnp.arange(col_count, dtype=jnp.int32)[None, :]
        logits = jnp.dot(features, head_part, preferred_element_type=jnp.float32)
        masked = jnp.where(allowed, logits, masked_value)
        chosen = jnp.sum(jnp.where(hit, logits, 0.0), axis=1)
        return allowed, hit, masked, chosen

    views = [view(head, own_list, place), view(far_head, far_list, other)]
    row_peak = jnp.maximum(jnp.max(views[0][2], axis=1), jnp.max(views[1][2], axis=1))
    row_total = sum(
        jnp.sum(jnp.where(v[0], jnp.exp(v[2] - row_peak[:, None]), 0.0), axis=1) for v in views
    )
    chosen = views[0][3] + views[1][3]
    stats = jnp.stack([row_peak, row_total, chosen])
    gathered = [stats] + [shift_within(stats, step) for step in range(1, group)]
    global_peak = gathered[0][0]
    for g in gathered[1:]:
        global_peak = jnp.maximum(global_peak, g[0])
    global_total = sum(g[1] * jnp.exp(g[0] - global_peak) for g in gathered)
    target_logit = sum(g[2] for g in gathered)
    logprob = target_logit - global_peak - jnp.log(global_total)
    expected_own, cand_coeff = candidate_terms(logprob, costs, seq_length)
    row_coeff = jnp.broadcast_to(
        cand_coeff[:, :, None], (sent_count, cand_count, seq_length)
    ).reshape(row_count)

    def grads(v):
        allowed, hit, masked, _ = v
        prob = jnp.where(allowed, jnp.exp(masked - global_peak[:, None]), 0.0) / global_total[:, None]
        return (row_coeff[:, None] * (hit.astype(jnp.float32) - prob)).astype(jnp.bfloat16)

    own_grad, far_grad = grads(views[0]), grads(views[1])

    expected_far = shift_half(expected_own)
    first = half == 0
    expected = jnp.concatenate(
        [jnp.where(first, expected_own, expected_far), jnp.where(first, expected_far, expected_own)]
    )

    mine = my_bit(1)
    split = features.reshape(row_count, dp_count // 2, 2, piece_rows)
    keep_features = lax.dynamic_slice_in_dim(split, mine, 1, 2).reshape(row_count, -1)
    send_features = lax.dynamic_slice_in_dim(split, 1 - mine, 1, 2).reshape(row_count, -1)

    def reduced(grad):
        def product(part):
            return lax.dot_general(
                part, grad, (((0,), (0,)), ((), ())), preferred_element_type=jnp.float32
            )

        received = swap_dp(product(send_features).astype(jnp.bfloat16), 1)
        total = product(keep_features) + received.astype(jnp.float32)
        width = col_count // 2
        parts = []
        for index, order in enumerate((wide, wide[::-1])):
            part = total[:, index * width : (index + 1) * width]
            part = part.reshape((2,) * len(wide) + (1, piece_rows, width))
            for bit in order:
                part = scatter_step(part, bit)
            parts.append(part.reshape(piece_rows, width))
        return jnp.concatenate(parts, axis=1)

    far_sum = shift_half(reduced(far_grad).astype(jnp.bfloat16))
    head_grad = reduced(own_grad) + far_sum.astype(jnp.float32)

    share = row_count // group

    def rows_grad(index):
        own = lax.dynamic_slice_in_dim(own_grad, index * share, share, 0)
        far = lax.dynamic_slice_in_dim(far_grad, index * share, share, 0)
        dims = (((1,), (1,)), ((), ()))
        return lax.dot_general(
            own, head, dims, preferred_element_type=jnp.float32
        ) + lax.dot_general(far, far_head, dims, preferred_element_type=jnp.float32)

    arrived = [
        shift_within(rows_grad((spot + step) % group).astype(jnp.bfloat16), step)
        for step in range(1, group)
    ]
    summed = rows_grad(spot)
    for value in arrived:
        summed = summed + value.astype(jnp.float32)
    return (summed.astype(jnp.bfloat16), head_grad, expected)


def body(hidden, head, shortlist, tokens, risk):
    vocab_count = lax.axis_size("vocab")
    dp_count = lax.axis_size("dp")
    splits = (
        vocab_count % 2 == 0
        and shortlist.shape[0] % 2 == 0
        and dp_count & (dp_count - 1) == 0
        and dp_count >= 4
        and head.shape[0] % dp_count == 0
        and (hidden.shape[0] // 2) % (vocab_count // 2) == 0
        and head.shape[1] % 2 == 0
    )
    return (halves if splits else plain)(hidden, head, shortlist, tokens, risk)


def solution(mesh):
    return jax.shard_map(
        body,
        mesh=mesh,
        in_specs=(P("dp", "vocab"), P(None, "vocab"), P("dp", "vocab"), P("dp"), P("dp", None)),
        out_specs=(P(("dp", "vocab"), None), P("dp", "vocab"), P("dp")),
        check_vma=False,
    )
```

```python
import functools

import jax
import jax.numpy as jnp
from jax import lax
from jax.experimental import pallas as pl
from jax.experimental.pallas import tpu as pltpu
from jax.sharding import PartitionSpec as P


masked_value = -1e30
loss_scale = 2048.0
kernel_vmem = 12 << 20


def add_pieces(received):
    return jnp.sum(received.astype(jnp.float32), axis=0)


def swap_dp(value, bit):
    count = lax.axis_size("dp")
    return lax.ppermute(value, "dp", [(i, i ^ bit) for i in range(count)])


def shift_half(value):
    count = lax.axis_size("vocab")
    return lax.ppermute(value, "vocab", [(i, (i + count // 2) % count) for i in range(count)])


def shift_within(value, step):
    count = lax.axis_size("vocab")
    group = count // 2
    pairs = [(i, i // group * group + (i % group + step) % group) for i in range(count)]
    return lax.ppermute(value, "vocab", pairs)


def after(value, *others):
    return lax.optimization_barrier((value,) + others)[0]


def dp_bits():
    count = lax.axis_size("dp")
    return [1 << b for b in range(count.bit_length() - 1)]


def plain(hidden, head, shortlist, tokens, risk):
    features = lax.all_gather(hidden, "vocab", axis=1, tiled=True)
    row_count = features.shape[0]
    sent_count = shortlist.shape[0]
    cand_count = risk.shape[1]
    per_sentence = row_count // sent_count
    seq_length = per_sentence // cand_count
    col_count = head.shape[1]
    block_width = col_count // shortlist.shape[1]
    col_offset = lax.axis_index("vocab") * col_count
    expanded = jnp.repeat(shortlist, block_width, axis=1) == 1
    allowed = jnp.broadcast_to(expanded[:, None, :], (sent_count, per_sentence, col_count)).reshape(
        row_count, col_count
    )
    target_hit = (tokens - col_offset)[:, None] == jnp.arange(col_count, dtype=jnp.int32)[None, :]
    logits = jnp.dot(features, head, preferred_element_type=jnp.float32)
    masked = jnp.where(allowed, logits, masked_value)
    row_peak = jnp.max(masked, axis=1)
    row_total = jnp.sum(jnp.where(allowed, jnp.exp(masked - row_peak[:, None]), 0.0), axis=1)
    chosen = jnp.sum(jnp.where(target_hit, logits, 0.0), axis=1)
    global_peak = lax.pmax(row_peak, "vocab")
    global_total, target_logit = lax.psum(
        (row_total * jnp.exp(row_peak - global_peak), chosen), "vocab"
    )
    logprob = target_logit - global_peak - jnp.log(global_total)
    expected, cand_coeff = candidate_terms(logprob, risk, seq_length)
    row_coeff = jnp.broadcast_to(
        cand_coeff[:, :, None], (sent_count, cand_count, seq_length)
    ).reshape(row_count)
    row_prob = (
        jnp.where(allowed, jnp.exp(masked - global_peak[:, None]), 0.0) / global_total[:, None]
    )
    grad_logits = (row_coeff[:, None] * (target_hit.astype(jnp.float32) - row_prob)).astype(
        jnp.bfloat16
    )
    model_width = features.shape[1]
    vocab_count = lax.axis_size("vocab")
    share_rows = row_count // vocab_count
    partial_value = (
        lax.dot_general(
            grad_logits, head, (((1,), (1,)), ((), ())), preferred_element_type=jnp.float32
        )
        .astype(jnp.bfloat16)
        .reshape(vocab_count, share_rows, model_width)
    )
    summed = add_pieces(
        lax.all_to_all(partial_value, "vocab", split_axis=0, concat_axis=0, tiled=True)
    )
    head_grad = lax.psum_scatter(
        lax.dot_general(
            features, grad_logits, (((0,), (0,)), ((), ())), preferred_element_type=jnp.float32
        ).astype(jnp.bfloat16),
        "dp",
        scatter_dimension=0,
        tiled=True,
    ).astype(jnp.float32)
    return (summed.astype(jnp.bfloat16), head_grad, expected)


def candidate_terms(logprob, risk, seq_length):
    sent_count, cand_count = risk.shape
    scores = jnp.mean(logprob.reshape(sent_count, cand_count, seq_length), axis=2)
    raised = jnp.exp(scores)
    weights = raised / jnp.sum(raised, axis=1, keepdims=True)
    cost_value = risk.astype(jnp.float32) / 100.0
    expected = jnp.sum(weights * cost_value, axis=1)
    coeff = loss_scale * weights * (cost_value - expected[:, None]) / seq_length
    return expected, coeff


def column(row_vector, length):
    return jnp.transpose(jnp.broadcast_to(row_vector, (8, length)))[:, 0:1]


def row_stats(flags, words, totals):
    rows = totals[0].shape[0]
    widths = [t.shape[1] for t in totals]
    count = len(totals)
    col_count = widths[0]
    block_width = 2 * col_count // flags.shape[0] if flags.shape[0] else col_count

    def kernel(flags_ref, words_ref, *refs):
        logit_refs, out_ref = refs[:count], refs[count]
        peak = jnp.full((rows, 1), masked_value, jnp.float32)
        spot = column(words_ref[...], rows)
        start = 0
        pieces = []
        for ref in logit_refs:
            for b in range(ref.shape[1] // block_width):
                logits = ref[:, b * block_width : (b + 1) * block_width]
                listed = flags_ref[start // block_width] == 1
                pieces.append((ref, b, start, listed))
                top = jnp.max(logits, axis=1, keepdims=True)
                peak = jnp.where(listed, jnp.maximum(peak, top), peak)
                start += block_width
        total = jnp.zeros((rows, 1), jnp.float32)
        chosen = jnp.zeros((rows, 1), jnp.float32)
        for ref, b, begin, listed in pieces:
            logits = ref[:, b * block_width : (b + 1) * block_width]
            part = jnp.sum(jnp.exp(jnp.minimum(logits - peak, 0.0)), axis=1, keepdims=True)
            total = jnp.where(listed, total + part, total)
            lanes = lax.broadcasted_iota(jnp.int32, (rows, block_width), 1) + begin
            chosen += jnp.sum(
                jnp.where(spot == lanes.astype(jnp.float32), logits, 0.0), axis=1, keepdims=True
            )
        lane = lax.broadcasted_iota(jnp.int32, (rows, 128), 1)
        table = jnp.where(lane == 0, peak, jnp.where(lane == 1, total, chosen))
        out_ref[...] = jnp.transpose(table)[0:8, :]

    return pl.pallas_call(
        kernel,
        out_shape=jax.ShapeDtypeStruct((8, rows), jnp.float32),
        in_specs=[pl.BlockSpec(memory_space=pltpu.SMEM)]
        + [pl.BlockSpec(memory_space=pltpu.VMEM)] * (1 + count),
        out_specs=pl.BlockSpec(memory_space=pltpu.VMEM),
        compiler_params=pltpu.CompilerParams(vmem_limit_bytes=kernel_vmem),
        cost_estimate=pl.CostEstimate(
            flops=8 * rows * sum(widths),
            bytes_accessed=4 * rows * sum(widths),
            transcendentals=rows * sum(widths),
        ),
        name="row_stats",
    )(flags, words, *totals)


def row_grads(flags, words, costs, stats, totals, seq_length):
    rows = totals[0].shape[0]
    count = len(totals)
    peers = len(stats)
    cand_count = costs.shape[0]
    widths = [t.shape[1] for t in totals]
    block_width = 2 * widths[0] // flags.shape[0]
    padded = -(-cand_count // 8) * 8

    def kernel(flags_ref, words_ref, costs_ref, *refs):
        stat_refs, logit_refs = refs[:peers], refs[peers : peers + count]
        out_refs = refs[peers + count : peers + 2 * count]
        turned_refs, expected_ref = refs[peers + 2 * count : -1], refs[-1]
        peaks = [r[0:1, :] for r in stat_refs]
        peak = functools.reduce(jnp.maximum, peaks)
        total = sum(r[1:2, :] * jnp.exp(p - peak) for r, p in zip(stat_refs, peaks))
        target = sum(r[2:3, :] for r in stat_refs)
        logprob = target - peak - jnp.log(total)
        row_of = lax.broadcasted_iota(jnp.int32, (padded, rows), 1)
        first = lax.broadcasted_iota(jnp.int32, (padded, rows), 0) * seq_length
        belongs = (row_of >= first) & (row_of < first + seq_length)
        scores = jnp.sum(jnp.where(belongs, logprob, 0.0), axis=1, keepdims=True) / seq_length
        real = lax.broadcasted_iota(jnp.int32, (padded, 1), 0) < cand_count
        raised = jnp.where(real, jnp.exp(scores), 0.0)
        weights = raised / jnp.sum(raised, axis=0, keepdims=True)
        lanes = lax.broadcasted_iota(jnp.int32, (padded, 128), 1)
        subs = lax.broadcasted_iota(jnp.int32, (padded, 128), 0)
        risks = jnp.broadcast_to(costs_ref[0:1, :], (padded, 128))
        cost = jnp.sum(jnp.where(lanes == subs, risks, 0.0), axis=1, keepdims=True) / 100.0
        expected = jnp.sum(weights * cost, axis=0, keepdims=True)
        coeff = loss_scale * weights * (cost - expected) / seq_length
        row_coeff = jnp.sum(jnp.where(belongs, coeff, 0.0), axis=0, keepdims=True)
        expected_ref[...] = jnp.broadcast_to(expected, (1, 128))
        place = lax.broadcasted_iota(jnp.int32, (8, rows), 0)
        table = jnp.where(
            place == 0,
            peak,
            jnp.where(place == 1, total, jnp.where(place == 2, row_coeff, words_ref[...])),
        )
        turned = jnp.transpose(table)
        peak_col, total_col = turned[:, 0:1], turned[:, 1:2]
        coeff_col, spot = turned[:, 2:3], turned[:, 3:4]
        begin = 0
        for ref, out_ref, turned_ref in zip(logit_refs, out_refs, turned_refs):
            for b in range(ref.shape[1] // block_width):
                cols = slice(b * block_width, (b + 1) * block_width)
                listed = (flags_ref[begin // block_width] == 1).astype(jnp.float32)
                shifted = jnp.minimum(ref[:, cols] - peak_col, 0.0)
                prob = jnp.exp(shifted) / total_col * listed
                lane = lax.broadcasted_iota(jnp.int32, (rows, block_width), 1) + begin
                hit = (spot == lane.astype(jnp.float32)).astype(jnp.float32)
                value = coeff_col * (hit - prob)
                out_ref[:, cols] = value.astype(jnp.bfloat16)
                turned_ref[cols, :] = jnp.transpose(value).astype(jnp.bfloat16)
                begin += block_width

    vmem = pl.BlockSpec(memory_space=pltpu.VMEM)
    outs = pl.pallas_call(
        kernel,
        out_shape=[jax.ShapeDtypeStruct((rows, w), jnp.bfloat16) for w in widths]
        + [jax.ShapeDtypeStruct((w, rows), jnp.bfloat16) for w in widths]
        + [jax.ShapeDtypeStruct((1, 128), jnp.float32)],
        in_specs=[pl.BlockSpec(memory_space=pltpu.SMEM)] + [vmem] * (2 + peers + count),
        out_specs=[vmem] * (2 * count + 1),
        compiler_params=pltpu.CompilerParams(vmem_limit_bytes=kernel_vmem),
        cost_estimate=pl.CostEstimate(
            flops=8 * rows * sum(widths),
            bytes_accessed=6 * rows * sum(widths),
            transcendentals=rows * sum(widths),
        ),
        name="row_grads",
    )(flags, words, jnp.pad(costs.astype(jnp.float32), (0, 128 - cand_count))[None], *stats, *totals)
    return outs[:count], outs[count:-1], outs[-1]


def send_product(turned, features, order, piece):
    columns, rows = turned.shape
    count = len(order)

    def kernel(order_ref, turned_ref, in_ref, out_ref):
        left = turned_ref[...]
        for i in range(count):
            at = pl.multiple_of(order_ref[i] * piece, piece)
            value = jnp.dot(left, in_ref[:, pl.ds(at, piece)], preferred_element_type=jnp.float32)
            out_ref[:, i * piece : (i + 1) * piece] = value.astype(jnp.bfloat16)

    vmem = pl.BlockSpec(memory_space=pltpu.VMEM)
    return pl.pallas_call(
        kernel,
        out_shape=jax.ShapeDtypeStruct((columns, count * piece), jnp.bfloat16),
        in_specs=[pl.BlockSpec(memory_space=pltpu.SMEM), vmem, vmem],
        out_specs=vmem,
        compiler_params=pltpu.CompilerParams(vmem_limit_bytes=kernel_vmem),
        cost_estimate=pl.CostEstimate(
            flops=2 * rows * columns * count * piece,
            bytes_accessed=2 * (rows + columns) * count * piece,
            transcendentals=0,
        ),
        name="send_product",
    )(jnp.stack(order).astype(jnp.int32), turned, features)


def keep_product(turned, features, order, piece, received, places):
    columns, rows = turned.shape
    count = len(order)
    width = columns // 2
    middle = count // 2

    def kernel(order_ref, turned_ref, in_ref, got_ref, *out_refs):
        left = turned_ref[...]
        for i in range(count):
            at = pl.multiple_of(order_ref[i] * piece, piece)
            value = jnp.dot(left, in_ref[:, pl.ds(at, piece)], preferred_element_type=jnp.float32)
            value = value + got_ref[:, i * piece : (i + 1) * piece].astype(jnp.float32)
            for k in range(2):
                part = value[k * width : (k + 1) * width]
                at = places[k][i]
                spot = slice(at % middle * piece, (at % middle + 1) * piece)
                if at >= middle:
                    out_refs[k][:, spot] = part.astype(jnp.bfloat16)
                else:
                    out_refs[2 + k][:, spot] = part

    vmem = pl.BlockSpec(memory_space=pltpu.VMEM)
    return pl.pallas_call(
        kernel,
        out_shape=[jax.ShapeDtypeStruct((width, middle * piece), jnp.bfloat16)] * 2
        + [jax.ShapeDtypeStruct((width, middle * piece), jnp.float32)] * 2,
        in_specs=[pl.BlockSpec(memory_space=pltpu.SMEM), vmem, vmem, vmem],
        out_specs=[vmem] * 4,
        compiler_params=pltpu.CompilerParams(vmem_limit_bytes=kernel_vmem),
        cost_estimate=pl.CostEstimate(
            flops=2 * rows * columns * count * piece,
            bytes_accessed=2 * (rows + 3 * columns) * count * piece,
            transcendentals=0,
        ),
        name="keep_product",
    )(jnp.stack(order).astype(jnp.int32), turned, features, received)


def dot(left, right, dims):
    return lax.dot_general(left, right, (dims, ((), ())), preferred_element_type=jnp.float32)


def masks_of(bits):
    masks = [0]
    for bit in reversed(bits):
        masks = masks + [m | bit for m in masks]
    return masks


def halves(hidden, head, shortlist, tokens, risk):
    vocab_count = lax.axis_size("vocab")
    group = vocab_count // 2
    dp_count = lax.axis_size("dp")
    place = lax.axis_index("vocab")
    member = lax.axis_index("dp")
    half = place // group
    spot = place % group
    row_count = hidden.shape[0] // 2
    slice_width = hidden.shape[1]
    model_width, col_count = head.shape
    cand_count = risk.shape[1]
    seq_length = row_count // cand_count
    other = (place + group) % vocab_count
    bits = dp_bits()
    wide = bits[1:]
    orders = (wide, wide[::-1])
    piece_rows = model_width // dp_count
    width = col_count // 2
    cut = slice_width // 2

    first_row = member * piece_rows
    held = [
        shift_half(lax.dynamic_slice(head, (first_row, i * width), (piece_rows, width)))
        for i in range(2)
    ]
    own_rows = lax.dynamic_slice_in_dim(hidden, half * row_count, row_count, 0)
    neighbours = [shift_within(own_rows, step) for step in range(1, group)]
    far_list = shift_half(lax.dynamic_slice_in_dim(shortlist, 1 - half, 1, 0))
    far_rows = lax.dynamic_slice_in_dim(hidden, (1 - half) * row_count, row_count, 0)
    crossed = []
    for i in range(2):
        sent = after(far_rows[:, i * cut : (i + 1) * cut], held[i])
        crossed.append(shift_half(sent))
    masks = [[0], [0]]
    held = [h[None] for h in held]
    for level in range(len(wide)):
        for k in range(2):
            bit = orders[k][level]
            received = swap_dp(held[k], bit)
            held[k] = jnp.concatenate([held[k], received], axis=0)
            masks[k] = masks[k] + [m ^ bit for m in masks[k]]
    crossed = [after(c, *held) for c in crossed]
    relayed = [[shift_within(c, step) for step in range(1, group)] for c in crossed]
    far_head = jnp.zeros((model_width, col_count), jnp.bfloat16)
    for k in range(2):
        received = swap_dp(held[k], 1)
        for blocks, flip in ((held[k], 0), (received, 1)):
            for block, mask in zip(blocks, masks[k]):
                far_head = lax.dynamic_update_slice(
                    far_head, block, ((member ^ (mask | flip)) * piece_rows, k * width)
                )

    sources = [half * group + (spot - step) % group for step in range(group)]
    far_sources = [(s + group) % vocab_count for s in sources]

    def put(features, block, source, part=0):
        return lax.dynamic_update_slice(features, block, (0, source * slice_width + part * cut))

    features = jnp.zeros((row_count, model_width), jnp.bfloat16)
    for block, source in zip([own_rows] + neighbours, sources):
        features = put(features, block, source)
    for i in range(2):
        features = put(features, crossed[i], far_sources[0], i)
    for block, source in zip(relayed[0], far_sources[1:]):
        features = put(features, block, source, 0)
    for block, source in zip(relayed[1], far_sources[1:]):
        features = put(features, block, source, 1)
    totals = [dot(features, matrix, ((1,), (0,))) for matrix in (head, far_head)]

    own_list = lax.dynamic_slice_in_dim(shortlist, half, 1, 0)
    flags = jnp.concatenate([own_list[0], far_list[0]])
    words = lax.dynamic_slice_in_dim(tokens, half * row_count, row_count, 0)
    group_of = words // col_count
    within = words - group_of * col_count
    position = jnp.where(
        group_of == place, within, jnp.where(group_of == other, within + col_count, -1)
    ).astype(jnp.float32)[None]
    costs = lax.dynamic_slice_in_dim(risk, half, 1, 0)[0]
    stats = row_stats(flags, position, totals)
    gathered = [stats] + [shift_within(stats, step) for step in range(1, group)]
    (own_grad, far_grad), (own_turned, far_turned), expected_own = row_grads(
        flags, position, costs, gathered, totals, seq_length
    )

    order_masks = [masks_of(order) for order in orders]
    kept = order_masks[0]
    places = [[masks.index(m) for m in kept] for masks in order_masks]

    def core_step(turned):
        sent = send_product(turned, features, [member ^ m ^ 1 for m in kept], piece_rows)
        return swap_dp(sent, 1)

    def first_sends(turned, received):
        outs = keep_product(
            turned, features, [member ^ m for m in kept], piece_rows, received, places
        )
        return list(outs[:2]), list(outs[2:])

    def wide_steps(sends, keeps):
        for level in range(len(wide)):
            for k in range(2):
                got = swap_dp(sends[k], orders[k][level])
                total = keeps[k] + got.astype(jnp.float32)
                middle = total.shape[1] // 2
                if level + 1 < len(wide):
                    sends[k], keeps[k] = total[:, middle:].astype(jnp.bfloat16), total[:, :middle]
                else:
                    keeps[k] = total
        return jnp.concatenate(keeps, axis=0)

    far_parts = [far_turned[:width], far_turned[width:]]
    far_received = [core_step(t) for t in far_parts]
    far_first = [first_sends(t, r) for t, r in zip(far_parts, far_received)]

    share = row_count // group

    def turned_rows(value):
        pieces = [
            lax.dynamic_slice_in_dim(value, (spot + step) % group * share, share, 0)
            for step in range(1, group + 1)
        ]
        return jnp.concatenate(pieces, axis=0)

    rows_grad = (
        dot(turned_rows(own_grad), head, ((1,), (1,)))
        + dot(turned_rows(far_grad), far_head, ((1,), (1,)))
    ).astype(jnp.bfloat16)
    arrived = [
        shift_within(rows_grad[(step - 1) * share : step * share], step)
        for step in range(1, group)
    ]
    far_sums = [shift_half(wide_steps(*first).astype(jnp.bfloat16)) for first in far_first]
    own_received = core_step(own_turned)
    expected_far = shift_half(expected_own)
    first = half == 0
    expected = jnp.concatenate(
        [
            jnp.where(first, expected_own[0, :1], expected_far[0, :1]),
            jnp.where(first, expected_far[0, :1], expected_own[0, :1]),
        ]
    )
    own_sum = wide_steps(*first_sends(own_turned, own_received))
    far_sum = jnp.concatenate(far_sums, axis=0)
    head_grad = jnp.transpose(own_sum + far_sum.astype(jnp.float32))
    summed = rows_grad[(group - 1) * share :].astype(jnp.float32)
    for value in arrived:
        summed = summed + value.astype(jnp.float32)
    return (summed.astype(jnp.bfloat16), head_grad, expected)


def fits_halves(vocab_count, dp_count, hidden, head, shortlist, risk):
    return (
        vocab_count % 2 == 0
        and vocab_count >= 4
        and shortlist[0] == 2
        and dp_count & (dp_count - 1) == 0
        and dp_count == 2 * vocab_count
        and head[0] % (128 * dp_count) == 0
        and head[1] % 512 == 0
        and (head[1] // shortlist[1]) % 128 == 0
        and (head[1] // 2) % (head[1] // shortlist[1]) == 0
        and (hidden[0] // 2) % (8 * risk[1]) in range(8 * risk[1])
        and (hidden[0] // 2) % (vocab_count // 2) == 0
        and risk[1] <= 128
    )


def body(hidden, head, shortlist, tokens, risk):
    fits = fits_halves(
        lax.axis_size("vocab"),
        lax.axis_size("dp"),
        hidden.shape,
        head.shape,
        shortlist.shape,
        risk.shape,
    )
    return (halves if fits else plain)(hidden, head, shortlist, tokens, risk)


def solution(mesh):
    return jax.shard_map(
        body,
        mesh=mesh,
        in_specs=(P("dp", "vocab"), P(None, "vocab"), P("dp", "vocab"), P("dp"), P("dp", None)),
        out_specs=(P(("dp", "vocab"), None), P("dp", "vocab"), P("dp")),
        check_vma=False,
    )
```
